32 devices in a mesh: dp: 4 (over z), expert: 8 (over y, x, core).
Axes of the slice: x: 2, y: 2, z: 4, core: 2. Of those that a mesh axis runs over, the one named last changes fastest.
Arguments:
- layer_input: bfloat16 [16384, 768], P(('dp', 'expert')), may hold values from -6 to 6
- seq_lengths: int32 [32], P(('dp', 'expert')), may hold values from 64 to 512, as said below
- routes: int32 [16384, 2], P(('dp', 'expert')), may hold values from 0 to 9, all different within a row
- ln1_gain: float32 [768], replicated, may hold values from 0.25 to 1.75
- w_query: bfloat16 [768, 768], replicated, may hold values from -0.21875 to 0.21875
- w_key: bfloat16 [768, 768], replicated, may hold values from -0.21875 to 0.21875
- w_value: bfloat16 [768, 768], replicated, may hold values from -0.21875 to 0.21875
- w_output: bfloat16 [768, 768], replicated, may hold values from -0.625 to 0.625
- ln2_gain: float32 [768], replicated, may hold values from 0.25 to 1.75
- w_router: float32 [768, 10], replicated, may hold values from -0.15625 to 0.15625
- frozen_in: bfloat16 [2, 768, 3072], replicated, may hold values from -0.21875 to 0.21875
- frozen_out: bfloat16 [2, 3072, 768], replicated, may hold values from -0.15625 to 0.15625
- new_in: bfloat16 [8, 768, 3072], P('expert'), may hold values from -0.21875 to 0.21875
- new_out: bfloat16 [8, 3072, 768], P('expert'), may hold values from -0.15625 to 0.15625
- cotangent: bfloat16 [16384, 768], P(('dp', 'expert')), may hold values from -6 to 6
Outputs:
- output: float32 [16384, 768], P(('dp', 'expert'))
- grad_input: float32 [16384, 768], P(('dp', 'expert'))
- grad_ln1: float32 [768], replicated
- grad_w_query: float32 [768, 768], replicated
- grad_w_key: float32 [768, 768], replicated
- grad_w_value: float32 [768, 768], replicated
- grad_w_output: float32 [768, 768], replicated
- grad_ln2: float32 [768], replicated
- grad_router: float32 [768, 10], replicated
- grad_new_in: float32 [8, 768, 3072], P('expert', None, 'dp')
- grad_new_out: float32 [8, 3072, 768], P('expert', 'dp')
The draws below stay inside these ranges and needn't reach their ends.
Inputs may be any that keep to these rules, and one draw needn't show every extreme that they name: `seq_lengths`: in every draw one sequence has exactly 512 valid tokens and another exactly 64. `routes`: the two experts of a token differ.
All inputs are finite; a program needn't handle non-finite values.
Results may differ from the reference program's by a relative error of at most 0.013.
Values may be sent and summed in bfloat16 or wider, within the bound.
A program may use at most 192 MiB of HBM per device.

```python
from functools import partial
import jax
import jax.numpy as jnp
from jax import lax

D = 768
HEADS = 12
HEAD_DIM = 64
FF = 3072
TOK_DEV = 512
MIN_LEN = 64
FROZEN = 2
NEW = 8
EXPERTS = 10
CAP = 102
SEQS = 32
TOKENS = 16384


def draw_seq_lengths(key, part):
    base_lengths = jax.random.randint(jax.random.fold_in(key, 11), (SEQS,), MIN_LEN, TOK_DEV + 1)
    longest = jax.random.randint(jax.random.fold_in(key, 12), (), 0, SEQS)
    offset_value = jax.random.randint(jax.random.fold_in(key, 13), (), 1, SEQS)
    shortest = (longest + offset_value) % SEQS
    position = jnp.arange(SEQS, dtype=jnp.int32)
    lengths_out = jnp.where(position == longest, TOK_DEV, base_lengths)
    lengths_out = jnp.where(position == shortest, MIN_LEN, lengths_out)
    return lengths_out.astype(jnp.int32)


def block_scale(own_key, dims, cuts, smallest, high):
    def one(axis_at, blocks):
        draws = jax.random.uniform(jax.random.fold_in(jax.random.fold_in(own_key, 6), axis_at), (blocks,), jnp.float32, smallest / len(cuts), high / len(cuts))
        return jnp.repeat(jnp.exp(draws), dims[axis_at] // blocks).reshape((-1,) + (1,) * (len(dims) - axis_at - 1))

    loudness = one(*cuts[0])
    for cut in cuts[1:]:
        loudness = loudness * one(*cut)
    return loudness


def choose_distinct(stream_key, rows, number_of, top, lift):
    ranking = jax.random.permutation(jax.random.fold_in(stream_key, 1), number_of)
    favour = ranking
    for power in range(3):
        favour = favour * favour // number_of
    favour = favour * lift // number_of
    chance = jax.random.randint(jax.random.fold_in(stream_key, 2), (rows, number_of), 0, 4096) + favour
    holders = jax.random.permutation(jax.random.fold_in(stream_key, 3), rows)[jnp.arange(number_of) % rows]
    chance = jnp.where(jnp.arange(rows)[:, None] == holders[None, :], 1 << 14, chance)
    score = chance * number_of + jnp.arange(number_of)
    return lax.top_k(score.astype(jnp.int32), top)[1].astype(jnp.int32)


def bell_draw(stream_key, dims, scale, limit, shards=(), kind=jnp.bfloat16):
    result = jax.random.normal(stream_key, dims, jnp.float32) * scale
    if len(shards) > 0:
        result = block_scale(stream_key, dims, shards, -0.22, 0.18) * result
    return jnp.clip(result, min=-limit, max=limit).astype(kind)


def setup_inputs(seed: int = 0) -> dict:
    streams_of = jax.random.split(jax.random.key(seed), 16)
    layer_input = bell_draw(streams_of[0], (TOKENS, D), 1.0, 6.0, ((0, 32),))
    seq_lengths = draw_seq_lengths(jax.random.fold_in(streams_of[15], 71), 0)
    routes = choose_distinct(streams_of[2], TOKENS, EXPERTS, 2, 1638)
    ln1_gain = jnp.clip(1.0 + 0.15 * jax.random.normal(streams_of[3], (D,), jnp.float32), 0.25, 1.75)
    w_query = bell_draw(streams_of[4], (D, D), D ** -0.5, 0.21875)
    w_key = bell_draw(streams_of[5], (D, D), D ** -0.5, 0.21875)
    w_value = bell_draw(streams_of[6], (D, D), D ** -0.5, 0.21875)
    w_output = bell_draw(streams_of[7], (D, D), (D // 8) ** -0.5, 0.625)
    ln2_gain = jnp.clip(1.0 + 0.15 * jax.random.normal(streams_of[8], (D,), jnp.float32), 0.25, 1.75)
    w_router = bell_draw(streams_of[9], (D, EXPERTS), (2 * D) ** -0.5, 0.15625, (), jnp.float32)
    frozen_in = bell_draw(streams_of[10], (FROZEN, D, FF), D ** -0.5, 0.21875)
    frozen_out = bell_draw(streams_of[11], (FROZEN, FF, D), (FF // 2) ** -0.5, 0.15625)
    new_in = bell_draw(streams_of[12], (NEW, D, FF), D ** -0.5, 0.21875, ((0, 8),))
    new_out = bell_draw(streams_of[13], (NEW, FF, D), (FF // 2) ** -0.5, 0.15625, ((0, 8),))
    cotangent = bell_draw(streams_of[14], (TOKENS, D), 1.0, 6.0, ((0, 32),))
    return dict(layer_input=layer_input, seq_lengths=seq_lengths, routes=routes, ln1_gain=ln1_gain, w_query=w_query, w_key=w_key, w_value=w_value, w_output=w_output, ln2_gain=ln2_gain, w_router=w_router, frozen_in=frozen_in, frozen_out=frozen_out, new_in=new_in, new_out=new_out, cotangent=cotangent)


@jax.custom_vjp
def low(v):
    return lax.optimization_barrier(v.astype(jnp.bfloat16)).astype(jnp.float32)

@jax.custom_vjp
def low_back(v):
    return v

def low_keep(v):
    return (low(v), None)

def low_pass(kept, grad):
    return (grad,)

def back_keep(v):
    return (v, None)

def back_low(kept, grad):
    return (low(grad),)
low.defvjp(low_keep, low_pass)
low_back.defvjp(back_keep, back_low)
NORM_EPS = 1e-05
GELU_SCALE = 0.7978845608028654
GELU_CUBIC = 0.044715
MASK_VALUE = -1e+30

def matmul_high(left, right):
    return jnp.dot(left, right, precision=lax.Precision.HIGHEST, preferred_element_type=jnp.float32)

def layer_norm(values, gain):
    center = values - lax.optimization_barrier(jnp.mean(values, -1, keepdims=True))
    return center * lax.rsqrt(lax.optimization_barrier(jnp.mean(center * center, -1, keepdims=True)) + NORM_EPS) * gain

def gelu_value(values):
    return 0.5 * values * (1.0 + jnp.tanh(GELU_SCALE * (values + GELU_CUBIC * values * values * values)))

def route_slots(route_rows, length, capacity, new_count):
    tokens = route_rows.shape[0]
    pair_route = jnp.concatenate([route_rows[:, 0], route_rows[:, 1]])
    position = jnp.arange(tokens, dtype=jnp.int32)
    valid = position < length
    pair_valid = jnp.concatenate([valid, valid])
    expert_new = pair_route - FROZEN
    onehot = ((expert_new[:, None] == jnp.arange(new_count, dtype=jnp.int32)[None, :]) & pair_valid[:, None]).astype(jnp.int32)
    before = jnp.cumsum(onehot, 0, dtype=jnp.int32) - onehot
    rank = lax.optimization_barrier(jnp.sum(before * onehot, 1, dtype=jnp.int32))
    is_new = lax.optimization_barrier(jnp.sum(onehot, 1, dtype=jnp.int32)) > 0
    kept_new = is_new & (rank < capacity)
    slot = jnp.where(kept_new, expert_new * capacity + rank, -1).astype(jnp.int32)
    match = slot[None, :] == jnp.arange(new_count * capacity, dtype=jnp.int32)[:, None]
    filled = jnp.any(match, 1)
    slot_pair = lax.optimization_barrier(jnp.sum(jnp.where(match, jnp.arange(2 * tokens, dtype=jnp.int32)[None, :], 0), 1, dtype=jnp.int32))
    return (valid, kept_new, slot, filled, slot_pair)

def attend_one(packed):
    query_rows, key_rows, value_rows, length = packed
    tokens = query_rows.shape[0]
    head_query = query_rows.reshape(tokens, HEADS, HEAD_DIM)
    head_key = key_rows.reshape(tokens, HEADS, HEAD_DIM)
    head_value = value_rows.reshape(tokens, HEADS, HEAD_DIM)
    position = jnp.arange(tokens, dtype=jnp.int32)
    allowed = (position[None, :] <= position[:, None]) & (position[None, :] < length)
    scores = jnp.einsum('qhd,khd->hqk', head_query, head_key, precision=lax.Precision.HIGHEST) * HEAD_DIM ** (-0.5)
    scores = low_back(jnp.where(allowed[None], scores, MASK_VALUE))
    peak_value = lax.optimization_barrier(jnp.max(scores, -1, keepdims=True))
    expo_values = jnp.exp(scores - peak_value)
    probs = low(expo_values / lax.optimization_barrier(jnp.sum(expo_values, -1, keepdims=True)))
    mixed = jnp.einsum('hqk,khd->qhd', probs, head_value, precision=lax.Precision.HIGHEST)
    return mixed.reshape(tokens, HEADS * HEAD_DIM)

def reference(layer_input, seq_lengths, routes, ln1_gain, w_query, w_key, w_value, w_output, ln2_gain, w_router, frozen_in, frozen_out, new_in, new_out, cotangent):
    frozen_first = frozen_in.astype(jnp.float32)
    frozen_second = frozen_out.astype(jnp.float32)
    route_dev = routes.reshape(SEQS, TOK_DEV, 2)
    valid, kept_new, slot, filled, slot_pair = jax.vmap(partial(route_slots, capacity=CAP, new_count=NEW))(route_dev, seq_lengths)
    valid_all = valid.reshape(TOKENS).astype(jnp.float32)
    route_hot = (routes[:, :, None] == jnp.arange(EXPERTS, dtype=jnp.int32)[None, None, :]).astype(jnp.float32)
    slot_token = slot_pair % TOK_DEV
    safe_slot = jnp.maximum(slot, 0)

    def expert_new(packed):
        rows_expert, first_w, second_w = packed
        pre_values = low_back(matmul_high(rows_expert, first_w))
        act_values = low(gelu_value(pre_values))
        return low(low_back(matmul_high(act_values, second_w)))

    def mixture_of_experts(normed_two, router_w, expert_first, expert_second):
        expert_input = low(normed_two)
        logits = matmul_high(normed_two, router_w)
        peak_value = lax.optimization_barrier(jnp.max(logits, -1, keepdims=True))
        expo_values = jnp.exp(logits - peak_value)
        prob = expo_values / lax.optimization_barrier(jnp.sum(expo_values, -1, keepdims=True))
        chosen = lax.optimization_barrier(jnp.sum(route_hot * prob[:, None, :], -1))
        gates = chosen / lax.optimization_barrier(jnp.sum(chosen, 1, keepdims=True))
        frozen_weight = lax.optimization_barrier(jnp.sum(route_hot[:, :, :FROZEN] * gates[:, :, None], 1)) * valid_all[:, None]
        mixture = jnp.zeros((TOKENS, D), jnp.float32)
        for frozen_index in range(FROZEN):
            pre_values = low_back(matmul_high(expert_input, frozen_first[frozen_index]))
            act_values = low(gelu_value(pre_values))
            result_rows = low_back(matmul_high(act_values, frozen_second[frozen_index]))
            mixture = mixture + frozen_weight[:, frozen_index:frozen_index + 1] * result_rows
        input_dev = expert_input.reshape(SEQS, TOK_DEV, D)
        sent_rows = jax.vmap(lambda source_rows, row_index: source_rows[row_index])(input_dev, slot_token)
        sent_rows = low_back(jnp.where(filled[:, :, None], sent_rows, 0.0))
        grouped = sent_rows.reshape(SEQS, NEW, CAP, D).transpose(1, 0, 2, 3).reshape(NEW, SEQS * CAP, D)
        results = lax.map(expert_new, (grouped, expert_first, expert_second))
        result_dev = results.reshape(NEW, SEQS, CAP, D).transpose(1, 0, 2, 3).reshape(SEQS, NEW * CAP, D)
        pair_result = jax.vmap(lambda source_rows, row_index: source_rows[row_index])(result_dev, safe_slot)
        pair_result = jnp.where(kept_new[:, :, None], pair_result, 0.0)
        gates_dev = gates.reshape(SEQS, TOK_DEV, 2)
        pair_gate = jnp.concatenate([gates_dev[:, :, 0], gates_dev[:, :, 1]], 1)
        weighted = pair_gate[:, :, None] * pair_result
        return mixture + (weighted[:, :TOK_DEV] + weighted[:, TOK_DEV:]).reshape(TOKENS, D)

    def forward(inputs, gain_one, query_w, key_w, value_w, output_w, gain_two, router_w, expert_first, expert_second):
        normed_one = low(layer_norm(inputs, gain_one))
        query_rows = low(low_back(matmul_high(normed_one, query_w)))
        key_rows = low(low_back(matmul_high(normed_one, key_w)))
        value_rows = low(low_back(matmul_high(normed_one, value_w)))
        mixed = lax.map(jax.checkpoint(attend_one), (query_rows.reshape(SEQS, TOK_DEV, D), key_rows.reshape(SEQS, TOK_DEV, D), value_rows.reshape(SEQS, TOK_DEV, D), seq_lengths))
        merged = low(low_back(mixed.reshape(TOKENS, D)))
        hidden = inputs + low_back(matmul_high(merged, output_w))
        normed_two = layer_norm(hidden, gain_two)
        return hidden + mixture_of_experts(normed_two, router_w, expert_first, expert_second)
    output_value, pullback = jax.vjp(forward, layer_input.astype(jnp.float32), ln1_gain, w_query.astype(jnp.float32), w_key.astype(jnp.float32), w_value.astype(jnp.float32), w_output.astype(jnp.float32), ln2_gain, w_router, new_in.astype(jnp.float32), new_out.astype(jnp.float32))
    grads = pullback(cotangent.astype(jnp.float32))
    return (output_value, grads[0], grads[1], grads[2], grads[3], grads[4], grads[5], grads[6], grads[7], grads[8], grads[9])
```

```python
import functools

import jax
import jax.numpy as jnp
from jax import lax
from jax.experimental import pallas as pl
from jax.experimental.pallas import tpu as pltpu
from jax.sharding import PartitionSpec as P

HEADS = 12
FROZEN = 2
NORM_EPS = 1e-05
GELU_SCALE = 0.7978845608028654
GELU_CUBIC = 0.044715
MASK_VALUE = -1e30

F32 = jnp.float32
BF16 = jnp.bfloat16
NN = ((1,), (0,))
NT = ((1,), (1,))
TN = ((0,), (0,))
GROUP = 256
MESH = pl.DeviceIdType.MESH
VMEM_LIMIT = 56 * 1024 * 1024


def mm(left, right, dims, precision=None):
    return lax.dot_general(
        left, right, (dims, ((), ())), precision=precision, preferred_element_type=F32
    )


def iota(shape, axis, kind=jnp.int32):
    return lax.broadcasted_iota(jnp.int32, shape, axis).astype(kind)


def normalize(values):
    center = values - jnp.mean(values, -1, keepdims=True)
    factor = lax.rsqrt(jnp.mean(center * center, -1, keepdims=True) + NORM_EPS)
    return (center * factor, factor)


def norm_back(grad_normed, normed, factor):
    return factor * (
        grad_normed
        - jnp.mean(grad_normed, -1, keepdims=True)
        - normed * jnp.mean(grad_normed * normed, -1, keepdims=True)
    )


def gelu_both(values):
    square = values * values
    tangent = jnp.tanh(values * (GELU_SCALE + (GELU_SCALE * GELU_CUBIC) * square))
    half = 0.5 * values
    slope = (
        0.5
        + 0.5 * tangent
        + half * (1.0 - tangent * tangent) * (GELU_SCALE + (3.0 * GELU_SCALE * GELU_CUBIC) * square)
    )
    return (half + half * tangent, slope)


def call(kernel, outs, grid, in_specs, out_specs, scratch=(), name=None, flops=0, prefetch=0, **params):
    cost = pl.CostEstimate(flops=flops, bytes_accessed=flops // 400, transcendentals=0) if flops else None
    return pl.pallas_call(
        kernel,
        out_shape=outs,
        grid_spec=pltpu.PrefetchScalarGridSpec(
            num_scalar_prefetch=prefetch,
            grid=grid,
            in_specs=in_specs,
            out_specs=out_specs,
            scratch_shapes=list(scratch),
        ),
        name=name,
        cost_estimate=cost,
        compiler_params=pltpu.CompilerParams(vmem_limit_bytes=VMEM_LIMIT, **params),
    )


def full(shape):
    return pl.BlockSpec(shape, lambda *_: (0,) * len(shape), pipeline_mode=pl.Buffered(1))


def kept(shape):
    return pl.BlockSpec(shape, lambda *_: (0,) * len(shape))


def greet():
    barrier = pltpu.get_barrier_semaphore()
    count = lax.axis_size("expert")
    me = lax.axis_index("expert")

    @pl.loop(1, count)
    def _(ahead):
        pl.semaphore_signal(
            barrier, inc=1, device_id={"expert": lax.rem(me + ahead, count)}, device_id_type=MESH
        )

    pl.semaphore_wait(barrier, count - 1)


def exchange_copy(source, target, sems, ahead):
    count = lax.axis_size("expert")
    me = lax.axis_index("expert")
    to = lax.rem(me + ahead, count)
    return pltpu.make_async_remote_copy(
        src_ref=source.at[to],
        dst_ref=target.at[me],
        send_sem=sems.at[0, ahead],
        recv_sem=sems.at[1, ahead],
        device_id={"expert": to},
        device_id_type=MESH,
    )


def own_copy(source, target, sems):
    me = lax.axis_index("expert")
    return pltpu.make_async_copy(source.at[me], target.at[me], sems.at[0, 0])


def exchange_start(*moves):
    for move in moves:
        own_copy(*move).start()

    @pl.loop(1, lax.axis_size("expert"))
    def _(ahead):
        for move in moves:
            exchange_copy(*move, ahead).start()


def exchange_wait(*moves):
    for move in moves:
        own_copy(*move).wait()

    @pl.loop(1, lax.axis_size("expert"))
    def _(ahead):
        for move in moves:
            exchange_copy(*move, ahead).wait()


def mask_bias(bias_ref, length):
    tokens = bias_ref.shape[0]

    @pl.loop(0, tokens // 64)
    def _(at):
        rows = pl.ds(pl.multiple_of(at * 64, 64), 64)
        key_at = iota((64, tokens), 0) + at * 64
        query_at = iota((64, tokens), 1)
        allowed = (key_at <= query_at) & (key_at < length)
        bias_ref[rows, :] = jnp.where(allowed, 0.0, MASK_VALUE)


def forward_kernel(
    capacity,
    padded,
    new_count,
    length_ref,
    x_ref,
    gain1_ref,
    wq_ref,
    wk_ref,
    wv_ref,
    wo_ref,
    gain2_ref,
    router_ref,
    routes_ref,
    c_ref,
    q_ref,
    k_ref,
    v_ref,
    merged_ref,
    lse_ref,
    hidden_ref,
    expert_in_ref,
    normed_one_ref,
    prob_ref,
    aux_ref,
    columns_ref,
    far_c_ref,
    bias_ref,
    mixed_ref,
    normed_two_ref,
    send_ref,
    sems,
):
    step = pl.program_id(0)
    tokens, width = x_ref.shape
    head_dim = width // HEADS
    group_heads = GROUP // head_dim
    length = length_ref[0]
    row_block = 128

    valid = (iota((1, tokens), 1) < length).astype(F32)
    route0 = routes_ref[0:1, :]
    route1 = routes_ref[1:2, :]

    @pl.when(step == 0)
    def _():
        greet()
        new_at = iota((new_count, tokens), 0) + FROZEN
        hot0 = jnp.where(new_at == route0, valid, 0.0)
        hot1 = jnp.where(new_at == route1, valid, 0.0)
        earlier = (iota((tokens, tokens), 0) < iota((tokens, tokens), 1)).astype(F32).astype(BF16)
        before = mm(jnp.concatenate([hot0, hot1], 0).astype(BF16), earlier, NN)
        rank0 = jnp.sum(hot0 * before[:new_count], 0, keepdims=True)
        rank1 = jnp.sum(
            hot1 * (before[new_count:] + jnp.sum(hot0, 1, keepdims=True)), 0, keepdims=True
        )
        kept0 = (jnp.sum(hot0, 0, keepdims=True) > 0.0) & (rank0 < capacity)
        kept1 = (jnp.sum(hot1, 0, keepdims=True) > 0.0) & (rank1 < capacity)
        aux_ref[2:3, :] = jnp.where(kept0, (route0 - FROZEN).astype(F32) * padded + rank0, -1.0)
        aux_ref[3:4, :] = jnp.where(kept1, (route1 - FROZEN).astype(F32) * padded + rank1, -1.0)

        @pl.loop(0, new_count)
        def _(at):
            slot_at = iota((padded, tokens), 0, F32) + (at * padded).astype(F32)
            pick = (slot_at == aux_ref[2:3, :]) | (slot_at == aux_ref[3:4, :])
            pick = jnp.where(pick, 1.0, 0.0).astype(BF16)
            send_ref[at] = mm(pick, c_ref[...], NN).astype(BF16)

        exchange_start((send_ref, far_c_ref, sems))

    @pl.when(step == 0)
    def _():
        mask_bias(bias_ref, length)

        @pl.loop(0, tokens // row_block)
        def _(at):
            rows = pl.ds(pl.multiple_of(at * row_block, row_block), row_block)
            values = x_ref[rows, :].astype(F32)
            normed, _ = normalize(values)
            normed_one_ref[rows, :] = (normed * gain1_ref[...]).astype(BF16)
            hidden_ref[rows, :] = values

    normed_one = normed_one_ref[...]
    query = mm(normed_one, wq_ref[...], NN).astype(BF16)
    key = mm(normed_one, wk_ref[...], NN).astype(BF16)
    value = mm(normed_one, wv_ref[...], NN).astype(BF16)
    q_ref[...] = query
    k_ref[...] = key
    v_ref[...] = value
    value_t = value.astype(F32).T.astype(BF16)
    lane_head = iota((tokens, GROUP), 1) // head_dim
    scaled = query * jnp.asarray(head_dim ** (-0.5), BF16)
    half = tokens // 2
    for head in range(group_heads):
        own = jnp.where(lane_head == head, scaled, jnp.zeros_like(scaled))
        rows = slice(head * head_dim, (head + 1) * head_dim)
        for block in range(2):
            keys = half * (block + 1)
            columns = slice(block * half, (block + 1) * half)
            scores = mm(key[:keys], own[columns], NT) + bias_ref[:keys, columns]
            peak = jnp.max(scores, 0, keepdims=True)
            expo = jnp.exp(scores - peak)
            total = jnp.sum(expo, 0, keepdims=True)
            mixed = mm(value_t[rows, :keys], expo.astype(BF16), NN) * (1.0 / total)
            mixed_ref[rows, columns] = mixed
            lse_ref[pl.ds(step * group_heads + head, 1), columns] = peak + jnp.log(total)
    merged = mixed_ref[...].T.astype(BF16)
    merged_ref[...] = merged
    hidden_ref[...] += mm(merged, wo_ref[...], NN)

    @pl.when(step == pl.num_programs(0) - 1)
    def _():
        @pl.loop(0, tokens // row_block)
        def _(at):
            rows = pl.ds(pl.multiple_of(at * row_block, row_block), row_block)
            normed, _ = normalize(hidden_ref[rows, :])
            normed = normed * gain2_ref[...]
            normed_two_ref[rows, :] = normed
            expert_in_ref[rows, :] = normed.astype(BF16)

        logits = mm(router_ref[...], normed_two_ref[...], NT, lax.Precision.HIGHEST)
        expo = jnp.exp(logits - jnp.max(logits, 0, keepdims=True))
        prob = expo / jnp.sum(expo, 0, keepdims=True)
        prob_ref[...] = prob
        experts = prob.shape[0]
        expert_at = iota((experts, tokens), 0)
        chosen0 = jnp.sum(jnp.where(expert_at == route0, prob, 0.0), 0, keepdims=True)
        chosen1 = jnp.sum(jnp.where(expert_at == route1, prob, 0.0), 0, keepdims=True)
        chosen_total = chosen0 + chosen1
        gate0 = chosen0 / chosen_total
        gate1 = chosen1 / chosen_total
        weights = [
            valid * (jnp.where(route0 == f, gate0, 0.0) + jnp.where(route1 == f, gate1, 0.0))
            for f in range(FROZEN)
        ]
        zero = jnp.zeros_like(valid)
        table = jnp.concatenate(
            [gate0, gate1, aux_ref[2:3, :], aux_ref[3:4, :], weights[0], weights[1], chosen_total, valid]
            + [zero] * 120,
            0,
        )
        aux_ref[...] = table[:8]
        columns_ref[...] = table.T
        exchange_wait((send_ref, far_c_ref, sems))


def frozen_step(expert, x_ref, c_ref, columns_ref, win_ref, wout_ref, mix_in, rows_in, dots_in, mix_ref, rows_ref, dots_ref, grads_scr):
    step = pl.program_id(0)
    tokens = x_ref.shape[0]
    weight = columns_ref[:, 4 + expert : 5 + expert]

    @pl.when(step == 0)
    def _():
        grads_scr[...] = (weight * c_ref[...].astype(F32)).astype(BF16)

    rows = x_ref[...]
    grads = grads_scr[...]
    first_w = win_ref[0]
    second_w = wout_ref[0]
    act, slope = gelu_both(mm(rows, first_w, NN))
    act = act.astype(BF16)
    grad_pre = (mm(grads, second_w, NT) * slope).astype(BF16)
    res_part = mm(act, second_w, NN)
    rows_part = mm(grad_pre, first_w, NT)

    @pl.when(step == 0)
    def _():
        mix_ref[...] = res_part
        rows_ref[...] = rows_part if rows_in is None else rows_in[...] + rows_part

    @pl.when(step > 0)
    def _():
        mix_ref[...] += res_part
        rows_ref[...] += rows_part

    @pl.when(step == pl.num_programs(0) - 1)
    def _():
        result = mix_ref[...]
        dot = jnp.sum(result * c_ref[...].astype(F32), 1, keepdims=True)
        lane = iota((tokens, 128), 1)
        if mix_in is None:
            mix_ref[...] = weight * result
            dots_ref[...] = jnp.where(lane == expert, dot, 0.0)
        else:
            mix_ref[...] = mix_in[...] + weight * result
            dots_ref[...] = jnp.where(lane == expert, dot, dots_in[...])


def dispatch_kernel(
    x_ref,
    c_ref,
    columns_ref,
    aux_ref,
    win_ref,
    wout_ref,
    mix_ref,
    rows_ref,
    dots_ref,
    far_x_ref,
    far_gate_ref,
    grads_scr,
    send_ref,
    send_gate_ref,
    sems,
    gate_sems,
):
    step = pl.program_id(0)
    tokens = x_ref.shape[0]
    new_count, padded, _ = send_ref.shape
    moves = ((send_gate_ref, far_gate_ref, gate_sems), (send_ref, far_x_ref, sems))

    @pl.when(step == 0)
    def _():
        greet()

        @pl.loop(0, new_count)
        def _(at):
            slot_at = iota((128, tokens), 0, F32) + (at * padded).astype(F32)
            hit0 = slot_at == aux_ref[2:3, :]
            hit1 = slot_at == aux_ref[3:4, :]
            pick = jnp.where(hit0 | hit1, 1.0, 0.0).astype(BF16)
            gate = jnp.where(hit0, aux_ref[0:1, :], 0.0) + jnp.where(hit1, aux_ref[1:2, :], 0.0)
            gate = jnp.sum(gate, 1, keepdims=True)
            gate = jnp.where(iota((128, 128), 1) == 0, gate, 0.0).T
            send_ref[at] = mm(pick[:padded], x_ref[...], NN).astype(BF16)
            send_gate_ref[at] = gate[:8]

        exchange_start(*moves)

    frozen_step(
        0, x_ref, c_ref, columns_ref, win_ref, wout_ref, None, None, None, mix_ref, rows_ref, dots_ref, grads_scr
    )

    @pl.when(step == pl.num_programs(0) - 1)
    def _():
        exchange_wait(*moves)


def return_kernel(
    x_ref,
    c_ref,
    columns_ref,
    win_ref,
    wout_ref,
    mix_in,
    rows_in,
    dots_in,
    send_res_ref,
    send_rows_ref,
    mix_ref,
    rows_ref,
    dots_ref,
    back_res_ref,
    back_rows_ref,
    grads_scr,
    res_sems,
    rows_sems,
):
    step = pl.program_id(0)
    moves = ((send_res_ref, back_res_ref, res_sems), (send_rows_ref, back_rows_ref, rows_sems))

    @pl.when(step == 0)
    def _():
        greet()
        exchange_start(*moves)

    frozen_step(
        1, x_ref, c_ref, columns_ref, win_ref, wout_ref, mix_in, rows_in, dots_in, mix_ref, rows_ref, dots_ref, grads_scr
    )

    @pl.when(step == pl.num_programs(0) - 1)
    def _():
        exchange_wait(*moves)


def gated_rows(c_ref, gate_ref, out_ref, padded):
    @pl.loop(0, gate_ref.shape[0])
    def _(at):
        rows = pl.ds(pl.multiple_of(at * padded, 16), padded)
        tall = jnp.concatenate([gate_ref[at], jnp.zeros((120, 128), F32)], 0).T
        out_ref[rows, :] = (c_ref[rows, :].astype(F32) * tall[:padded, 0:1]).astype(BF16)


def home_kernel(
    padded, x_ref, c_ref, gate_ref, win_ref, wout_ref, res_ref, rows_ref, r_ref, act_ref, grad_pre_ref, res_acc, rows_acc
):
    step = pl.program_id(0)

    @pl.when(step == 0)
    def _():
        gated_rows(c_ref, gate_ref, r_ref, padded)

    rows = x_ref[...]
    grads = r_ref[...]
    first_w = win_ref[0]
    second_w = wout_ref[0]
    act, slope = gelu_both(mm(rows, first_w, NN))
    act = act.astype(BF16)
    grad_pre = (mm(grads, second_w, NT) * slope).astype(BF16)
    act_ref[0] = act
    grad_pre_ref[0] = grad_pre
    res_part = mm(act, second_w, NN)
    rows_part = mm(grad_pre, first_w, NT)

    @pl.when(step == 0)
    def _():
        res_acc[...] = res_part
        rows_acc[...] = rows_part

    @pl.when(step > 0)
    def _():
        res_acc[...] += res_part
        rows_acc[...] += rows_part

    @pl.when(step == pl.num_programs(0) - 1)
    def _():
        res_ref[...] = res_acc[...].astype(BF16)
        rows_ref[...] = rows_acc[...].astype(BF16)


def weight_grad_kernel(
    padded, order_ref, x_ref, r_ref, act_ref, grad_pre_ref, px_ref, pc_ref, pgate_ref, win_ref, wout_ref, dwin_ref, dwout_ref, pr_ref
):
    @pl.when(pl.program_id(0) == 0)
    def _():
        gated_rows(pc_ref, pgate_ref, pr_ref, padded)

    rows = px_ref[...]
    grads = pr_ref[...]
    act, slope = gelu_both(mm(rows, win_ref[0], NN))
    act = act.astype(BF16)
    grad_pre = (mm(grads, wout_ref[0], NT) * slope).astype(BF16)
    dwout = mm(act, grads, TN) + mm(act_ref[0], r_ref[...], TN)
    dwin = mm(rows, grad_pre, TN) + mm(x_ref[...], grad_pre_ref[0], TN)
    dwout_ref[0] = dwout.astype(dwout_ref.dtype)
    dwin_ref[0] = dwin.astype(dwin_ref.dtype)


def combine_kernel(
    res_ref,
    rows_ref,
    columns_ref,
    aux_ref,
    mix_ref,
    frozen_rows_ref,
    dots_ref,
    hidden_ref,
    c_ref,
    prob_ref,
    routes_ref,
    gain2_ref,
    router_ref,
    out_ref,
    grad_hidden_ref,
    grad_attn_ref,
    grad_ln2_ref,
    grad_router_ref,
):
    step = pl.program_id(0)
    block = hidden_ref.shape[0]
    slots = res_ref.shape[0]
    slot_at = iota((block, slots), 1, F32)
    pick0 = jnp.where(slot_at == columns_ref[:, 2:3], 1.0, 0.0)
    pick1 = jnp.where(slot_at == columns_ref[:, 3:4], 1.0, 0.0)
    pair0 = mm(pick0.astype(BF16), res_ref[...], NN)
    pair1 = mm(pick1.astype(BF16), res_ref[...], NN)
    grad_out = c_ref[...].astype(F32)
    hidden = hidden_ref[...]
    out_ref[...] = hidden + mix_ref[...] + columns_ref[:, 0:1] * pair0 + columns_ref[:, 1:2] * pair1
    dot0 = jnp.sum(grad_out * pair0, 1, keepdims=True)
    dot1 = jnp.sum(grad_out * pair1, 1, keepdims=True)
    lane = iota((block, 128), 1)
    dots = jnp.where(lane == FROZEN, dot0, jnp.where(lane == FROZEN + 1, dot1, dots_ref[...])).T
    valid = aux_ref[7:8, :]
    route0 = routes_ref[0:1, :]
    route1 = routes_ref[1:2, :]
    grad_gate0 = dots[FROZEN : FROZEN + 1]
    grad_gate1 = dots[FROZEN + 1 : FROZEN + 2]
    for f in range(FROZEN):
        grad_gate0 = grad_gate0 + jnp.where(route0 == f, valid * dots[f : f + 1], 0.0)
        grad_gate1 = grad_gate1 + jnp.where(route1 == f, valid * dots[f : f + 1], 0.0)
    mixing = grad_gate0 * aux_ref[0:1, :] + grad_gate1 * aux_ref[1:2, :]
    chosen_total = aux_ref[6:7, :]
    prob = prob_ref[...]
    experts = prob.shape[0]
    expert_at = iota((experts, block), 0)
    grad_prob = jnp.where(expert_at == route0, (grad_gate0 - mixing) / chosen_total, 0.0)
    grad_prob = grad_prob + jnp.where(expert_at == route1, (grad_gate1 - mixing) / chosen_total, 0.0)
    grad_logits = prob * (grad_prob - jnp.sum(prob * grad_prob, 0, keepdims=True))
    normed, factor = normalize(hidden)
    gain = gain2_ref[...]
    grad_router = mm(grad_logits, normed * gain, NN, lax.Precision.HIGHEST)
    grad_normed = (
        frozen_rows_ref[...]
        + mm((pick0 + pick1).astype(BF16), rows_ref[...], NN)
        + mm(grad_logits, router_ref[...], TN, lax.Precision.HIGHEST)
    )
    grad_ln2 = jnp.sum(grad_normed * normed, 0, keepdims=True)
    grad_hidden = grad_out + norm_back(grad_normed * gain, normed, factor)
    grad_hidden_ref[...] = grad_hidden
    grad_attn_ref[...] = grad_hidden.astype(BF16)

    @pl.when(step == 0)
    def _():
        grad_ln2_ref[...] = grad_ln2
        grad_router_ref[...] = grad_router

    @pl.when(step > 0)
    def _():
        grad_ln2_ref[...] += grad_ln2
        grad_router_ref[...] += grad_router


def backward_kernel(
    length_ref,
    x_ref,
    gain1_ref,
    normed_one_ref,
    q_ref,
    k_ref,
    v_ref,
    merged_ref,
    lse_ref,
    grad_attn_ref,
    grad_hidden_ref,
    wq_ref,
    wk_ref,
    wv_ref,
    wo_ref,
    dwq_ref,
    dwk_ref,
    dwv_ref,
    dwo_ref,
    grad_input_ref,
    grad_ln1_ref,
    bias_ref,
    grad_query_t,
    grad_key_ref,
    grad_value_ref,
):
    step = pl.program_id(0)
    tokens, width = x_ref.shape
    head_dim = width // HEADS
    group_heads = GROUP // head_dim
    scale = head_dim ** (-0.5)
    half = tokens // 2

    @pl.when(step == 0)
    def _():
        mask_bias(bias_ref, length_ref[0])

    grad_attn = grad_attn_ref[...]
    normed_one = normed_one_ref[...]
    query = q_ref[...]
    key = k_ref[...]
    value = v_ref[...]
    dwo_ref[...] = mm(merged_ref[...], grad_attn, TN).astype(dwo_ref.dtype)
    grad_merged = mm(grad_attn, wo_ref[...], NT).astype(BF16)
    key_t = key.astype(F32).T.astype(BF16)
    lane_head = iota((tokens, GROUP), 1) // head_dim
    scaled = query * jnp.asarray(scale, BF16)
    for head in range(group_heads):
        rows = slice(head * head_dim, (head + 1) * head_dim)
        own_query = jnp.where(lane_head == head, scaled, jnp.zeros_like(scaled))
        own_grad = jnp.where(lane_head == head, grad_merged, jnp.zeros_like(grad_merged))
        for block in range(2):
            keys = half * (block + 1)
            columns = slice(block * half, (block + 1) * half)
            scores = mm(key[:keys], own_query[columns], NT) + bias_ref[:keys, columns]
            lse = lse_ref[pl.ds(step * group_heads + head, 1), columns]
            prob = jnp.exp(scores - lse)
            grad_prob = mm(value[:keys], own_grad[columns], NT)
            delta = jnp.sum(prob * grad_prob, 0, keepdims=True)
            grad_scores = (prob * (grad_prob - delta)).astype(BF16)
            grad_query_t[rows, columns] = mm(key_t[rows, :keys], grad_scores, NN) * scale
            grad_value = mm(prob.astype(BF16), own_grad[columns], NN)
            grad_key = mm(grad_scores, own_query[columns], NN)
            if head == 0 and block == 0:
                grad_value_ref[:keys, :] = grad_value
                grad_key_ref[:keys, :] = grad_key
            elif head == 0:
                grad_value_ref[:half, :] += grad_value[:half]
                grad_key_ref[:half, :] += grad_key[:half]
                grad_value_ref[half:, :] = grad_value[half:]
                grad_key_ref[half:, :] = grad_key[half:]
            else:
                grad_value_ref[:keys, :] += grad_value
                grad_key_ref[:keys, :] += grad_key
    grad_query = grad_query_t[...].T.astype(BF16)
    grad_key = grad_key_ref[...].astype(BF16)
    grad_value = grad_value_ref[...].astype(BF16)
    dwq_ref[...] = mm(normed_one, grad_query, TN).astype(dwq_ref.dtype)
    dwk_ref[...] = mm(normed_one, grad_key, TN).astype(dwk_ref.dtype)
    dwv_ref[...] = mm(normed_one, grad_value, TN).astype(dwv_ref.dtype)
    part = (
        mm(grad_query, wq_ref[...], NT)
        + mm(grad_key, wk_ref[...], NT)
        + mm(grad_value, wv_ref[...], NT)
    )

    @pl.when(step == 0)
    def _():
        grad_input_ref[...] = part
        grad_ln1_ref[...] = jnp.zeros_like(grad_ln1_ref)

    @pl.when(step > 0)
    def _():
        grad_input_ref[...] += part

    @pl.when(step == pl.num_programs(0) - 1)
    def _():
        row_block = 128

        @pl.loop(0, tokens // row_block)
        def _(at):
            rows = pl.ds(pl.multiple_of(at * row_block, row_block), row_block)
            grad_normed = grad_input_ref[rows, :]
            normed, factor = normalize(x_ref[rows, :].astype(F32))
            grad_ln1_ref[...] += jnp.sum(grad_normed * normed, 0, keepdims=True)
            grad_input_ref[rows, :] = grad_hidden_ref[rows, :] + norm_back(
                grad_normed * gain1_ref[...], normed, factor
            )


def routes_of_sum():
    near = [("expert", 1 << at) for at in range((lax.axis_size("expert") - 1).bit_length())]
    deep = [("dp", 1 << at) for at in range((lax.axis_size("dp") - 1).bit_length())]
    first, middle = near[:1], near[1:]
    return [first + middle + deep, first + middle[::-1] + deep] * 3


def partner(axis, bit):
    return {axis: lax.axis_index(axis) ^ bit}


def sum_kernel(q_ref, k_ref, v_ref, o_ref, small_ref, all_ref, small_sum_ref, sum_ref, got_ref, small_got_ref, sems, small_sems):
    plans = routes_of_sum()
    phases = len(plans[0])
    rows = sum_ref.shape[0] // len(plans)
    barrier = pltpu.get_barrier_semaphore()
    for axis, bit in plans[0]:
        pl.semaphore_signal(barrier, inc=1, device_id=partner(axis, bit), device_id_type=MESH)
    width = q_ref.shape[0]
    for at, ref in enumerate((q_ref, k_ref, v_ref, o_ref)):
        sum_ref[at * width : (at + 1) * width, :] = ref[...]
    small_sum_ref[0] = small_ref[...]
    pl.semaphore_wait(barrier, phases)

    def place(plan, phase):
        start, size = 0, rows
        for axis, bit in plan[:phase]:
            size //= 2
            start = start + size * jnp.where((lax.axis_index(axis) & bit) != 0, 1, 0)
        return start, size

    def span(stream, start, size):
        return pl.ds(pl.multiple_of(stream * rows + start, 16), size)

    def scatter(stream, phase):
        plan = plans[stream]
        axis, bit = plan[phase]
        start, size = place(plan, phase)
        size //= 2
        other = start + size * jnp.where((lax.axis_index(axis) & bit) != 0, 0, 1)
        landing = stream * rows + rows - 2 * size
        return pltpu.make_async_remote_copy(
            src_ref=sum_ref.at[span(stream, other, size)],
            dst_ref=got_ref.at[pl.ds(landing, size)],
            send_sem=sems.at[0, phase, stream],
            recv_sem=sems.at[1, phase, stream],
            device_id=partner(axis, bit),
            device_id_type=MESH,
        )

    def add(stream, phase):
        start, size = place(plans[stream], phase + 1)
        landing = stream * rows + rows - 2 * size
        mine = span(stream, start, size)
        total = sum_ref[mine, :].astype(F32) + got_ref[landing : landing + size, :].astype(F32)
        into = all_ref if phase == phases - 1 else sum_ref
        into[mine, :] = total.astype(BF16)

    def spread(stream, phase):
        plan = plans[stream]
        axis, bit = plan[phase]
        start, size = place(plan, phase + 1)
        mine = span(stream, start, size)
        return pltpu.make_async_remote_copy(
            src_ref=all_ref.at[mine],
            dst_ref=all_ref.at[mine],
            send_sem=sems.at[0, phases + phase, stream],
            recv_sem=sems.at[1, phases + phase, stream],
            device_id=partner(axis, bit),
            device_id_type=MESH,
        )

    def small(phase):
        axis, bit = plans[0][phase]
        return pltpu.make_async_remote_copy(
            src_ref=small_sum_ref.at[phase],
            dst_ref=small_got_ref.at[phase],
            send_sem=small_sems.at[0, phase],
            recv_sem=small_sems.at[1, phase],
            device_id=partner(axis, bit),
            device_id_type=MESH,
        )

    streams = range(len(plans))
    small(0).start()
    for stream in streams:
        scatter(stream, 0).start()
    for phase in range(phases):
        small(phase).wait()
        small_sum_ref[phase + 1] = small_sum_ref[phase] + small_got_ref[phase]
        if phase + 1 < phases:
            small(phase + 1).start()
        for stream in streams:
            scatter(stream, phase).wait()
            add(stream, phase)
            if phase + 1 < phases:
                scatter(stream, phase + 1).start()
            else:
                spread(stream, phase).start()
    for phase in reversed(range(phases)):
        for stream in streams:
            spread(stream, phase).wait()
            if phase > 0:
                spread(stream, phase - 1).start()


def sum_all(q, k, v, o, small):
    width = q.shape[0]
    plans = routes_of_sum()
    phases = len(plans[0])
    whole = pl.BlockSpec(memory_space=pltpu.VMEM)
    shape = jax.ShapeDtypeStruct
    total, small_total = pl.pallas_call(
        sum_kernel,
        out_shape=(shape((4 * width, width), BF16), shape((phases + 1,) + small.shape, F32)),
        in_specs=[whole] * 5,
        out_specs=(whole, whole),
        scratch_shapes=[
            pltpu.VMEM((4 * width, width), BF16),
            pltpu.VMEM((4 * width, width), BF16),
            pltpu.VMEM((phases,) + small.shape, F32),
            pltpu.SemaphoreType.DMA((2, 2 * phases, len(plans))),
            pltpu.SemaphoreType.DMA((2, phases)),
        ],
        name="sum_all",
        compiler_params=pltpu.CompilerParams(
            vmem_limit_bytes=VMEM_LIMIT, collective_id=3, has_side_effects=True
        ),
    )(q, k, v, o, small)
    return total, small_total[phases]


def on_device(
    layer_input,
    seq_lengths,
    routes,
    ln1_gain,
    w_query,
    w_key,
    w_value,
    w_output,
    ln2_gain,
    w_router,
    frozen_in,
    frozen_out,
    new_in,
    new_out,
    cotangent,
):
    tokens, width = layer_input.shape
    hidden_units = frozen_in.shape[2]
    copies = lax.axis_size("dp")
    new_count = new_in.shape[0] * lax.axis_size("expert")
    experts = FROZEN + new_count
    capacity = 2 * tokens // experts
    padded = -(-capacity // 16) * 16
    slots = new_count * padded
    groups = width // GROUP
    shape = jax.ShapeDtypeStruct
    smem = pl.BlockSpec(memory_space=pltpu.SMEM)
    gain1 = ln1_gain.reshape(1, width)
    gain2 = ln2_gain.reshape(1, width)
    router_t = w_router.T
    routes_t = routes.T
    by_column = pl.BlockSpec((width, GROUP), lambda i: (0, i))
    by_row = pl.BlockSpec((GROUP, width), lambda i: (i, 0))
    by_group = pl.BlockSpec((tokens, GROUP), lambda i: (0, i))
    act_shape = shape((tokens, width), BF16)
    wide_shape = shape((tokens, width), F32)
    sent_shape = shape((new_count, padded, width), BF16)
    gate_shape = shape((new_count, 8, 128), F32)
    table_shape = shape((tokens, 128), F32)
    anywhere = pl.BlockSpec(memory_space=pl.ANY)
    exchange_sems = pltpu.SemaphoreType.DMA((2, lax.axis_size("expert")))
    share = hidden_units // copies

    (query, key, value, merged, lse, hidden, expert_in, normed_one, prob, aux, columns, far_c) = call(
        functools.partial(forward_kernel, capacity, padded, new_count),
        (
            act_shape,
            act_shape,
            act_shape,
            act_shape,
            shape((HEADS, tokens), F32),
            wide_shape,
            act_shape,
            act_shape,
            shape((experts, tokens), F32),
            shape((8, tokens), F32),
            shape((tokens, 128), F32),
            sent_shape,
        ),
        (groups,),
        [
            smem,
            full((tokens, width)),
            full((1, width)),
            by_column,
            by_column,
            by_column,
            by_row,
            full((1, width)),
            full((experts, width)),
            full((2, tokens)),
            full((tokens, width)),
        ],
        (
            by_group,
            by_group,
            by_group,
            by_group,
            kept((HEADS, tokens)),
            kept((tokens, width)),
            kept((tokens, width)),
            kept((tokens, width)),
            kept((experts, tokens)),
            kept((8, tokens)),
            kept((tokens, 128)),
            anywhere,
        ),
        [
            pltpu.VMEM((tokens, tokens), F32),
            pltpu.VMEM((GROUP, tokens), F32),
            pltpu.VMEM((tokens, width), F32),
            pltpu.VMEM((new_count, padded, width), BF16),
            exchange_sems,
        ],
        name="attend_forward",
        flops=12 * tokens * width * width,
        collective_id=0,
        has_side_effects=True,
    )(
        seq_lengths,
        layer_input,
        gain1,
        w_query,
        w_key,
        w_value,
        w_output,
        gain2,
        router_t,
        routes_t,
        cotangent,
    )

    chunk = 768
    frozen_flops = 8 * tokens * width * hidden_units
    frozen_specs = [full((tokens, width)), full((tokens, width)), full((tokens, 128))]

    def frozen_weights(f):
        return [
            pl.BlockSpec((1, width, chunk), lambda i: (f, 0, i)),
            pl.BlockSpec((1, chunk, width), lambda i: (f, i, 0)),
        ]

    frozen_outs = (wide_shape, wide_shape, table_shape)
    frozen_out_specs = (kept((tokens, width)), kept((tokens, width)), kept((tokens, 128)))
    mix, frozen_rows, dots, far_x, far_gate = call(
        dispatch_kernel,
        frozen_outs + (sent_shape, gate_shape),
        (hidden_units // chunk,),
        frozen_specs + [full((8, tokens))] + frozen_weights(0),
        frozen_out_specs + (anywhere, anywhere),
        [
            pltpu.VMEM((tokens, width), BF16),
            pltpu.VMEM((new_count, padded, width), BF16),
            pltpu.VMEM((new_count, 8, 128), F32),
            exchange_sems,
            exchange_sems,
        ],
        name="dispatch",
        flops=frozen_flops,
        collective_id=1,
        has_side_effects=True,
    )(expert_in, cotangent, columns, aux, frozen_in, frozen_out)
    far_x = far_x.reshape(slots, width)
    far_c = far_c.reshape(slots, width)

    me = lax.axis_index("dp")
    beside = [(i, i ^ 1) for i in range(copies)]
    pair_c = lax.ppermute(far_c, "dp", beside)
    pair_x = lax.ppermute(far_x, "dp", beside)
    pair_gate = lax.ppermute(far_gate, "dp", beside)

    row_shape = shape((slots, width), BF16)
    kept_shape = shape((copies, slots, share), BF16)
    by_share = pl.BlockSpec((1, slots, share), lambda i: (i, 0, 0))
    new_res, new_rows, far_r, act, grad_pre = call(
        functools.partial(home_kernel, padded),
        (row_shape, row_shape, row_shape, kept_shape, kept_shape),
        (copies,),
        [
            full((slots, width)),
            full((slots, width)),
            full((new_count, 8, 128)),
            pl.BlockSpec((1, width, share), lambda i: (0, 0, i)),
            pl.BlockSpec((1, share, width), lambda i: (0, i, 0)),
        ],
        (kept((slots, width)), kept((slots, width)), kept((slots, width)), by_share, by_share),
        [pltpu.VMEM((slots, width), F32), pltpu.VMEM((slots, width), F32)],
        name="new_experts",
        flops=8 * slots * width * hidden_units,
    )(far_x, far_c, far_gate, new_in, new_out)

    def weight_grads(order, kind):
        steps = len(order)
        picked = lambda i, o: (o[i], 0, 0)
        return call(
            functools.partial(weight_grad_kernel, padded),
            (shape((steps, width, share), kind), shape((steps, share, width), kind)),
            (steps,),
            [
                full((slots, width)),
                full((slots, width)),
                pl.BlockSpec((1, slots, share), picked),
                pl.BlockSpec((1, slots, share), picked),
                full((slots, width)),
                full((slots, width)),
                full((new_count, 8, 128)),
                pl.BlockSpec((1, width, share), lambda i, o: (0, 0, o[i])),
                pl.BlockSpec((1, share, width), lambda i, o: (0, o[i], 0)),
            ],
            (
                pl.BlockSpec((1, width, share), lambda i, o: (i, 0, 0)),
                pl.BlockSpec((1, share, width), lambda i, o: (i, 0, 0)),
            ),
            [pltpu.VMEM((slots, width), BF16)],
            name="weight_grads",
            prefetch=1,
            flops=12 * slots * width * share * steps,
        )(
            jnp.stack(order).astype(jnp.int32),
            far_x,
            far_r,
            act,
            grad_pre,
            pair_x,
            pair_c,
            pair_gate,
            new_in,
            new_out,
        )

    ahead = range(2, copies, 2)
    sent_in, sent_out = weight_grads([lax.rem(me + k, copies) for k in ahead], BF16)
    sent_in, sent_out, new_res = lax.optimization_barrier((sent_in, sent_out, new_res))
    own_in, own_out = weight_grads([me], F32)
    grad_new_in, grad_new_out = own_in, own_out
    for at, k in enumerate(ahead):
        shift = [(i, (i + k) % copies) for i in range(copies)]
        got_out = lax.ppermute(sent_out[at], "dp", shift)
        got_in = lax.ppermute(sent_in[at], "dp", shift)
        grad_new_out = grad_new_out + got_out.astype(F32)[None]
        grad_new_in = grad_new_in + got_in.astype(F32)[None]

    mix, frozen_rows, dots, returned, grad_back = call(
        return_kernel,
        frozen_outs + (sent_shape, sent_shape),
        (hidden_units // chunk,),
        frozen_specs
        + frozen_weights(1)
        + [full((tokens, width)), full((tokens, width)), full((tokens, 128)), anywhere, anywhere],
        frozen_out_specs + (anywhere, anywhere),
        [pltpu.VMEM((tokens, width), BF16), exchange_sems, exchange_sems],
        name="return_rows",
        flops=frozen_flops,
        collective_id=2,
        has_side_effects=True,
    )(
        expert_in,
        cotangent,
        columns,
        frozen_in,
        frozen_out,
        mix,
        frozen_rows,
        dots,
        new_res.reshape(new_count, padded, width),
        new_rows.reshape(new_count, padded, width),
    )
    returned = returned.reshape(slots, width)
    grad_back = grad_back.reshape(slots, width)

    block = 256
    rows_of = lambda lanes: pl.BlockSpec((block, lanes), lambda i: (i, 0))
    lanes_of = lambda rows: pl.BlockSpec((rows, block), lambda i: (0, i))
    output, grad_hidden, grad_attn, grad_ln2, grad_router = call(
        combine_kernel,
        (
            wide_shape,
            wide_shape,
            act_shape,
            shape((1, width), F32),
            shape((experts, width), F32),
        ),
        (tokens // block,),
        [
            full((slots, width)),
            full((slots, width)),
            rows_of(128),
            lanes_of(8),
            rows_of(width),
            rows_of(width),
            rows_of(128),
            rows_of(width),
            rows_of(width),
            lanes_of(experts),
            lanes_of(2),
            full((1, width)),
            full((experts, width)),
        ],
        (
            rows_of(width),
            rows_of(width),
            rows_of(width),
            kept((1, width)),
            kept((experts, width)),
        ),
        name="combine",
    )(
        returned,
        grad_back,
        columns,
        aux,
        mix,
        frozen_rows,
        dots,
        hidden,
        cotangent,
        prob,
        routes_t,
        gain2,
        router_t,
    )

    weight_shape = shape((width, width), BF16)
    dwq, dwk, dwv, dwo, grad_input, grad_ln1 = call(
        backward_kernel,
        (
            weight_shape,
            weight_shape,
            weight_shape,
            weight_shape,
            wide_shape,
            shape((1, width), F32),
        ),
        (groups,),
        [
            smem,
            full((tokens, width)),
            full((1, width)),
            full((tokens, width)),
            by_group,
            by_group,
            by_group,
            by_group,
            full((HEADS, tokens)),
            full((tokens, width)),
            full((tokens, width)),
            by_column,
            by_column,
            by_column,
            by_row,
        ],
        (
            by_column,
            by_column,
            by_column,
            by_row,
            kept((tokens, width)),
            kept((1, width)),
        ),
        [
            pltpu.VMEM((tokens, tokens), F32),
            pltpu.VMEM((GROUP, tokens), F32),
            pltpu.VMEM((tokens, GROUP), F32),
            pltpu.VMEM((tokens, GROUP), F32),
        ],
        name="attend_backward",
    )(
        seq_lengths,
        layer_input,
        gain1,
        normed_one,
        query,
        key,
        value,
        merged,
        lse,
        grad_attn,
        grad_hidden,
        w_query,
        w_key,
        w_value,
        w_output,
    )
    small = jnp.concatenate([grad_ln1, grad_ln2, grad_router], 0)
    small = jnp.pad(small, ((0, -small.shape[0] % 8), (0, 0)))
    devices = copies * lax.axis_size("expert")
    if 4 * width % (6 * 16 * devices) == 0:
        total, small = sum_all(dwq, dwk, dwv, dwo, small)
        dwq, dwk, dwv, dwo = (total[i * width : (i + 1) * width] for i in range(4))
    else:
        dwq, dwk, dwv, dwo, small = lax.psum((dwq, dwk, dwv, dwo, small), ("dp", "expert"))
    return (
        output,
        grad_input,
        small[0],
        dwq.astype(F32),
        dwk.astype(F32),
        dwv.astype(F32),
        dwo.astype(F32),
        small[1],
        small[2 : 2 + experts].T,
        grad_new_in,
        grad_new_out,
    )


def solution(mesh):
    placed = (
        P(("dp", "expert"), None),
        P(("dp", "expert")),
        P(("dp", "expert"), None),
        P(),
        P(),
        P(),
        P(),
        P(),
        P(),
        P(),
        P(),
        P(),
        P("expert", None, None),
        P("expert", None, None),
        P(("dp", "expert"), None),
    )
    return jax.shard_map(
        on_device,
        mesh=mesh,
        in_specs=placed,
        out_specs=(
            P(("dp", "expert"), None),
            P(("dp", "expert"), None),
            P(),
            P(),
            P(),
            P(),
            P(),
            P(),
            P(),
            P("expert", None, "dp"),
            P("expert", "dp", None),
        ),
        check_vma=False,
    )
```
